256 devices in a mesh: row: 8 (over x, core), col: 32 (over z, y).
Axes of the slice: x: 4, y: 4, z: 8, core: 2. Of those that a mesh axis runs over, the one named last changes fastest.
Arguments:
- panel: bfloat16 [65536, 512], P('row', 'col'), may hold values from -0.0234375 to 0.0234375
- pheno: bfloat16 [65536, 8192], P('row', 'col'), may hold values from -48 to 48
- kin_values: float32 [512], replicated, may hold values from 0.1 to 10
- trait_values: float32 [128], replicated, may hold values from 0.1 to 10
- trait_basis: float32 [128, 128], replicated, may hold values from -0.5 to 0.5
Outputs:
- coeffs: float32 [512, 8192], P('row', 'col')
- genetic: bfloat16 [65536, 8192], P('row', 'col')
The draws below stay inside these ranges and needn't reach their ends.
All inputs are finite; a program needn't handle non-finite values.
Results may differ from the reference program's by a relative error of at most 0.0049.
Values may be sent and summed in bfloat16 or wider, within the bound.
No kernel may reach another device: no remote copies, remote signals or barrier semaphores. Data moves between devices by JAX's collectives and lax.ppermute only.
A program may use at most 64 MiB of HBM per device.

```python
import math
import jax
import jax.numpy as jnp
from jax import lax

PANEL = 512
TRAITS = 128
NIND = 65536
SETS = 64


def block_levels(key, dims, pieces, smallest, high):
    gain = 1.0
    for dim, blocks in pieces:
        draws = jax.random.uniform(jax.random.fold_in(jax.random.fold_in(key, 6), dim), (blocks,), jnp.float32, smallest / len(pieces), high / len(pieces))
        gain = gain * jnp.repeat(jnp.exp(draws), dims[dim] // blocks).reshape((-1,) + (1,) * (len(dims) - 1 - dim))
    return gain


def gaussian(rng, shape, width, bound, cuts=(), kind=jnp.bfloat16):
    values = jax.random.normal(rng, shape, jnp.float32) * width
    if len(cuts) > 0:
        values = block_levels(rng, shape, cuts, -0.22, 0.18) * values
    return jnp.clip(values, min=-bound, max=bound).astype(kind)


def setup_inputs(seed: int = 0) -> dict:
    key_list = jax.random.split(jax.random.key(seed), 6)
    panel = gaussian(key_list[0], (NIND, PANEL), NIND ** -0.5, 0.0234375, ((0, 8), (1, 32)))
    pheno = gaussian(key_list[1], (NIND, TRAITS * SETS), 8.0, 48.0, ((0, 8), (1, 32)))
    kin_values = jnp.clip(jnp.exp(jax.random.uniform(key_list[2], (PANEL,), jnp.float32, math.log(0.1), math.log(10.0))), 0.1, 10.0)
    trait_values = jnp.clip(jnp.exp(jax.random.uniform(key_list[3], (TRAITS,), jnp.float32, math.log(0.1), math.log(10.0))), 0.1, 10.0)
    trait_basis = gaussian(key_list[4], (TRAITS, TRAITS), TRAITS ** -0.5, 0.5, (), jnp.float32)
    return {"panel": panel, "pheno": pheno, "kin_values": kin_values, "trait_values": trait_values, "trait_basis": trait_basis}


def reference(panel, pheno, kin_values, trait_values, trait_basis):
    projected = jnp.dot(panel.T, pheno, preferred_element_type=jnp.float32)
    layered = projected.reshape(PANEL, TRAITS, SETS)
    rotated = jnp.einsum("pts,tj->psj", layered, trait_basis, precision=lax.Precision.HIGHEST)
    product = kin_values[:, None] * trait_values[None, :]
    scaled = rotated * (product / (product + 1.0))[:, None, :]
    unrotated = jnp.einsum("psj,tj->pts", scaled, trait_basis, precision=lax.Precision.HIGHEST)
    coeffs = unrotated.reshape(PANEL, TRAITS * SETS)
    genetic = jnp.dot(panel, coeffs.astype(jnp.bfloat16), preferred_element_type=jnp.float32)
    return coeffs, genetic.astype(jnp.bfloat16)
```

```python
import jax
import jax.numpy as jnp
from jax import lax
from jax.sharding import Mesh, PartitionSpec as P

ROW = ("x", "core")
COL = ("z", "y")
ALL = ROW + COL
NX, NC, NZ, NY = 4, 2, 8, 4
SHARE = 16
TRAITS = 128
SETS = 64
LA = 3328


def shift(value, axis, count, step):
    return lax.ppermute(value, axis, [(i, (i + step) % count) for i in range(count)])


def ring(own, axis, count):
    before, after = {0: own}, {0: own}
    for k in range(1, count // 2):
        before[-k] = shift(before[1 - k], axis, count, 1)
        after[k] = shift(after[k - 1], axis, count, -1)
    half = own.shape[1] // 256 * 128
    far = jnp.concatenate(
        [
            shift(before[1 - count // 2][:, :half], axis, count, 1),
            shift(after[count // 2 - 1][:, half:], axis, count, -1),
        ],
        axis=1,
    )
    return {k % count: v for k, v in {**before, **after, count // 2: far}.items()}


def gather_panel(own):
    a, b = {}, {}
    by_y = ring(own, "y", NY)
    for dy, block in by_y.items():
        b[dy, 0] = block[:, LA:]
    along = ring(jnp.concatenate([by_y[dy][:, :LA] for dy in range(NY)], 0), "z", NZ)
    for dz, block in along.items():
        for dy in range(NY):
            a[dy, dz] = block[dy * SHARE : (dy + 1) * SHARE]
    by_z = ring(own[:, LA:], "z", NZ)
    for near in ((7, 1, 6, 2), (5, 3, 4)):
        group = ring(jnp.concatenate([by_z[dz] for dz in near], 0), "y", NY)
        for dy, block in group.items():
            for n, dz in enumerate(near):
                b[dy, dz] = block[n * SHARE : (n + 1) * SHARE]
    order = [(dy, dz) for dy in range(NY) for dz in range(NZ)]
    return jnp.concatenate(
        [jnp.concatenate([a[k], b[k]], 1) for k in order], 0
    )


def turn(value, axis, by):
    count = value.shape[axis]
    twice = jnp.concatenate([value, value], axis)
    return lax.dynamic_slice_in_dim(twice, count - by, count, axis)


def local(panel, pheno, kin_values, trait_values, trait_basis):
    z, y = lax.axis_index("z"), lax.axis_index("y")
    row = lax.axis_index("x") * NC + lax.axis_index("core")
    whole = gather_panel(panel.T)
    part = jnp.dot(whole, pheno, preferred_element_type=jnp.float32)
    part = part.reshape(NY, NZ, SHARE, TRAITS // 32 * SETS)
    part = turn(turn(part, 1, z), 0, y).reshape(NY, 128, 4, SETS)
    outgoing = part.astype(jnp.bfloat16).transpose(3, 0, 2, 1).reshape(256, 4, 128)
    incoming = lax.all_to_all(outgoing, ALL, 0, 0, tiled=True)
    summed = jnp.sum(incoming.reshape(8, TRAITS, 128).astype(jnp.float32), 0)
    kin = lax.dynamic_index_in_dim(kin_values.reshape(NZ, NY, SHARE), y, 1, False)
    gain = trait_values[:, None] * kin.reshape(1, 128)
    high = lax.Precision.HIGHEST
    rotated = jnp.einsum("tj,tp->jp", trait_basis, summed, precision=high)
    scaled = rotated * (gain / (gain + 1.0))
    unrotated = jnp.einsum("tj,jp->tp", trait_basis, scaled, precision=high)
    low = unrotated.astype(jnp.bfloat16).reshape(1, 32, 4, 128)
    back = jnp.broadcast_to(low, (8, 32, 4, 128)).reshape(256, 4, 128)
    back = lax.all_to_all(back, ALL, 0, 0, tiled=True)
    coeffs_low = back.reshape(SETS, NY, 4, 128).transpose(1, 3, 2, 0)
    coeffs_low = coeffs_low.reshape(NY, NZ, SHARE, 256)
    coeffs = lax.dynamic_index_in_dim(coeffs_low, row, 1, False)
    coeffs = coeffs.reshape(NY * SHARE, 256).astype(jnp.float32)
    here = turn(turn(coeffs_low, 1, (NZ - z) % NZ), 0, (NY - y) % NY).reshape(512, 256)
    genetic = lax.dot_general(
        whole, here, (((0,), (0,)), ((), ())), preferred_element_type=jnp.float32
    )
    return coeffs, genetic.astype(jnp.bfloat16)


def solution(mesh):
    split = Mesh(mesh.devices.reshape(NX, NC, NZ, NY), ALL)
    return jax.shard_map(
        local,
        mesh=split,
        in_specs=(P(ROW, COL), P(ROW, COL), P(), P(), P()),
        out_specs=(P(ROW, COL), P(ROW, COL)),
        check_vma=False,
    )
```

```python
import jax
import jax.numpy as jnp
from jax import lax
from jax.sharding import Mesh, PartitionSpec as P

ROW = ("x", "core")
COL = ("z", "y")
ALL = ROW + COL
NX, NC, NZ, NY = 4, 2, 8, 4
SHARE = 16
TRAITS = 128
SETS = 64
LA = 3328


def shift(value, axis, count, step):
    return lax.ppermute(value, axis, [(i, (i + step) % count) for i in range(count)])


def pair(before, after, axis, count):
    return shift(before, axis, count, 1), shift(after, axis, count, -1)


def halves(before, after, axis, count):
    half = before.shape[1] // 256 * 128
    return shift(before[:, :half], axis, count, 1), shift(after[:, half:], axis, count, -1)


def tied(*values):
    return lax.optimization_barrier(values)


def gather_panel(own):
    b0 = own[:, LA:]
    b1 = pair(b0, b0, "z", NZ)
    o1 = pair(own, own, "y", NY)
    b2 = pair(*b1, "z", NZ)
    o2 = halves(*o1, "y", NY)
    *b2, o1a, o1b = tied(*b2, *o1)
    o1 = (o1a, o1b)
    b3 = pair(*b2, "z", NZ)
    p0 = jnp.concatenate([b1[0], b1[1], b2[0], b2[1]], 0)
    p1 = pair(p0, p0, "y", NY)
    far = jnp.concatenate(tied(*o2), 1)
    a0 = jnp.concatenate([v[:, :LA] for v in (own, o1[1], far, o1[0])], 0)
    a1 = pair(a0, a0, "z", NZ)
    b4 = jnp.concatenate(halves(*b3, "z", NZ), 1)
    a2 = pair(*a1, "z", NZ)
    q0 = jnp.concatenate([b3[0], b3[1], b4], 0)
    *p1, a1a, a1b, q0 = tied(*p1, *a1, q0)
    a1 = (a1a, a1b)
    p2 = jnp.concatenate(halves(*p1, "y", NY), 1)
    q1 = pair(q0, q0, "y", NY)
    *a2, p1a, p1b = tied(*a2, *p1)
    p1 = (p1a, p1b)
    a3 = pair(*a2, "z", NZ)
    *a3, p2 = tied(*a3, p2)
    a4 = jnp.concatenate(halves(*a3, "z", NZ), 1)
    q2 = jnp.concatenate(halves(*q1, "y", NY), 1)
    by_z = (a0, a1[1], a2[1], a3[1], a4, a3[0], a2[0], a1[0])
    a = {
        (dy, dz): by_z[dz][dy * SHARE : (dy + 1) * SHARE]
        for dy in range(NY)
        for dz in range(NZ)
    }
    b = {}
    for group, near in (
        ((own[:, LA:], o1[1][:, LA:], far[:, LA:], o1[0][:, LA:]), (0,)),
        ((p0, p1[1], p2, p1[0]), (7, 1, 6, 2)),
        ((q0, q1[1], q2, q1[0]), (5, 3, 4)),
    ):
        for dy in range(NY):
            for n, dz in enumerate(near):
                b[dy, dz] = group[dy][n * SHARE : (n + 1) * SHARE]
    order = [(dy, dz) for dy in range(NY) for dz in range(NZ)]
    return jnp.concatenate(
        [jnp.concatenate([a[k], b[k]], 1) for k in order], 0
    )


def turn(value, axis, by):
    count = value.shape[axis]
    twice = jnp.concatenate([value, value], axis)
    return lax.dynamic_slice_in_dim(twice, count - by, count, axis)


def local(panel, pheno, kin_values, trait_values, trait_basis):
    z, y = lax.axis_index("z"), lax.axis_index("y")
    row = lax.axis_index("x") * NC + lax.axis_index("core")
    whole = gather_panel(panel.T)
    part = jnp.dot(whole, pheno, preferred_element_type=jnp.float32)
    part = part.reshape(NY, NZ, SHARE, TRAITS // 32 * SETS)
    part = turn(turn(part, 1, z), 0, y).reshape(NY, 128, 4, SETS)
    outgoing = part.astype(jnp.bfloat16).transpose(3, 0, 2, 1).reshape(256, 4, 128)
    incoming = lax.all_to_all(outgoing, ALL, 0, 0, tiled=True)
    summed = jnp.sum(incoming.reshape(8, TRAITS, 128).astype(jnp.float32), 0)
    kin = lax.dynamic_index_in_dim(kin_values.reshape(NZ, NY, SHARE), y, 1, False)
    gain = trait_values[:, None] * kin.reshape(1, 128)
    high = lax.Precision.HIGHEST
    rotated = jnp.einsum("tj,tp->jp", trait_basis, summed, precision=high)
    scaled = rotated * (gain / (gain + 1.0))
    unrotated = jnp.einsum("tj,jp->tp", trait_basis, scaled, precision=high)
    low = unrotated.astype(jnp.bfloat16).reshape(1, 32, 4, 128)
    back = jnp.broadcast_to(low, (8, 32, 4, 128)).reshape(256, 4, 128)
    back = lax.all_to_all(back, ALL, 0, 0, tiled=True)
    coeffs_low = back.reshape(SETS, NY, 4, 128).transpose(1, 3, 2, 0)
    coeffs_low = coeffs_low.reshape(NY, NZ, SHARE, 256)
    coeffs = lax.dynamic_index_in_dim(coeffs_low, row, 1, False)
    coeffs = coeffs.reshape(NY * SHARE, 256).astype(jnp.float32)
    here = turn(turn(coeffs_low, 1, (NZ - z) % NZ), 0, (NY - y) % NY).reshape(512, 256)
    genetic = lax.dot_general(
        whole, here, (((0,), (0,)), ((), ())), preferred_element_type=jnp.float32
    )
    return coeffs, genetic.astype(jnp.bfloat16)


def solution(mesh):
    split = Mesh(mesh.devices.reshape(NX, NC, NZ, NY), ALL)
    return jax.shard_map(
        local,
        mesh=split,
        in_specs=(P(ROW, COL), P(ROW, COL), P(), P(), P()),
        out_specs=(P(ROW, COL), P(ROW, COL)),
        check_vma=False,
    )
```

```python
import jax
import jax.numpy as jnp
from jax import lax
from jax.sharding import Mesh, PartitionSpec as P

ROW = ("x", "core")
COL = ("z", "y")
ALL = ROW + COL
CHIPS = ("x",) + COL
NX, NC, NZ, NY = 4, 2, 8, 4
SHARE = 16
TRAITS = 128
SETS = 64
LA = 3328


def shift(value, axis, count, step):
    return lax.ppermute(value, axis, [(i, (i + step) % count) for i in range(count)])


def pair(before, after, axis, count):
    return shift(before, axis, count, 1), shift(after, axis, count, -1)


def halves(before, after, axis, count):
    half = before.shape[1] // 256 * 128
    return shift(before[:, :half], axis, count, 1), shift(after[:, half:], axis, count, -1)


def tied(*values):
    return lax.optimization_barrier(values)


def gather_panel(own):
    b0 = own[:, LA:]
    b1 = pair(b0, b0, "z", NZ)
    o1 = pair(own, own, "y", NY)
    b2 = pair(*b1, "z", NZ)
    o2 = halves(*o1, "y", NY)
    *b2, o1a, o1b = tied(*b2, *o1)
    o1 = (o1a, o1b)
    b3 = pair(*b2, "z", NZ)
    p0 = jnp.concatenate([b1[0], b1[1], b2[0], b2[1]], 0)
    p1 = pair(p0, p0, "y", NY)
    far = jnp.concatenate(tied(*o2), 1)
    a0 = jnp.concatenate([v[:, :LA] for v in (own, o1[1], far, o1[0])], 0)
    a1 = pair(a0, a0, "z", NZ)
    b4 = jnp.concatenate(halves(*b3, "z", NZ), 1)
    a2 = pair(*a1, "z", NZ)
    q0 = jnp.concatenate([b3[0], b3[1], b4], 0)
    *p1, a1a, a1b, q0 = tied(*p1, *a1, q0)
    a1 = (a1a, a1b)
    p2 = jnp.concatenate(halves(*p1, "y", NY), 1)
    q1 = pair(q0, q0, "y", NY)
    *a2, p1a, p1b = tied(*a2, *p1)
    p1 = (p1a, p1b)
    a3 = pair(*a2, "z", NZ)
    *a3, p2 = tied(*a3, p2)
    a4 = jnp.concatenate(halves(*a3, "z", NZ), 1)
    q2 = jnp.concatenate(halves(*q1, "y", NY), 1)
    by_z = (a0, a1[1], a2[1], a3[1], a4, a3[0], a2[0], a1[0])
    a = {
        (dy, dz): by_z[dz][dy * SHARE : (dy + 1) * SHARE]
        for dy in range(NY)
        for dz in range(NZ)
    }
    b = {}
    for group, near in (
        ((own[:, LA:], o1[1][:, LA:], far[:, LA:], o1[0][:, LA:]), (0,)),
        ((p0, p1[1], p2, p1[0]), (7, 1, 6, 2)),
        ((q0, q1[1], q2, q1[0]), (5, 3, 4)),
    ):
        for dy in range(NY):
            for n, dz in enumerate(near):
                b[dy, dz] = group[dy][n * SHARE : (n + 1) * SHARE]
    order = [(dy, dz) for dy in range(NY) for dz in range(NZ)]
    return jnp.concatenate(
        [jnp.concatenate([a[k], b[k]], 1) for k in order], 0
    )


def turn(value, axis, by):
    count = value.shape[axis]
    twice = jnp.concatenate([value, value], axis)
    return lax.dynamic_slice_in_dim(twice, count - by, count, axis)


def local(panel, pheno, kin_values, trait_values, trait_basis):
    z, y = lax.axis_index("z"), lax.axis_index("y")
    core = lax.axis_index("core")
    row = lax.axis_index("x") * NC + core
    whole = gather_panel(panel.T)
    part = jnp.dot(whole, pheno, preferred_element_type=jnp.float32)
    part = part.reshape(NY, NZ, SHARE, TRAITS // 32 * SETS)
    part = turn(part, 1, z)
    part = jnp.concatenate([part, part], 0)
    mine = lax.dynamic_slice_in_dim(part, (NC * core + NY - y) % NY, NC, 0)
    theirs = lax.dynamic_slice_in_dim(part, (NC * (1 - core) + NY - y) % NY, NC, 0)
    part = mine + shift(theirs, "core", NC, 1)
    part = part.reshape(NC, 128, 4, SETS)
    outgoing = part.astype(jnp.bfloat16).transpose(3, 0, 2, 1).reshape(128, 4, 128)
    incoming = lax.all_to_all(outgoing, CHIPS, 0, 0, tiled=True)
    summed = jnp.sum(incoming.reshape(NX, TRAITS, 128).astype(jnp.float32), 0)
    kin = lax.dynamic_index_in_dim(
        kin_values.reshape(NZ, NY, SHARE), NC * core + y % NC, 1, False
    )
    gain = trait_values[:, None] * kin.reshape(1, 128)
    high = lax.Precision.HIGHEST
    rotated = jnp.einsum("tj,tp->jp", trait_basis, summed, precision=high)
    scaled = rotated * (gain / (gain + 1.0))
    unrotated = jnp.einsum("tj,jp->tp", trait_basis, scaled, precision=high)
    low = unrotated.astype(jnp.bfloat16).reshape(1, 32, 4, 128)
    back = jnp.broadcast_to(low, (NX, 32, 4, 128)).reshape(128, 4, 128)
    back = lax.all_to_all(back, CHIPS, 0, 0, tiled=True)
    coeffs_low = back.reshape(SETS, NC, 4, 128).transpose(1, 3, 2, 0).reshape(256, 256)
    coeffs_low = jnp.concatenate([coeffs_low, shift(coeffs_low, "core", NC, 1)], 0)
    coeffs_low = coeffs_low.reshape(NY, NZ, SHARE, 256)
    coeffs = lax.dynamic_index_in_dim(coeffs_low, row, 1, False)
    coeffs = turn(coeffs, 0, NC * core).reshape(NY * SHARE, 256).astype(jnp.float32)
    here = turn(coeffs_low, 1, (NZ - z) % NZ)
    here = turn(here, 0, (NC * core + NY - y) % NY).reshape(512, 256)
    genetic = lax.dot_general(
        whole, here, (((0,), (0,)), ((), ())), preferred_element_type=jnp.float32
    )
    return coeffs, genetic.astype(jnp.bfloat16)


def solution(mesh):
    split = Mesh(mesh.devices.reshape(NX, NC, NZ, NY), ALL)
    return jax.shard_map(
        local,
        mesh=split,
        in_specs=(P(ROW, COL), P(ROW, COL), P(), P(), P()),
        out_specs=(P(ROW, COL), P(ROW, COL)),
        check_vma=False,
    )
```
